512 devices in a mesh: seq: 64 (over x, z), head: 8 (over y, core).
Axes of the slice: x: 4, y: 4, z: 16, core: 2. Of those that a mesh axis runs over, the one named last changes fastest.
Arguments:
- qk: bfloat16 [8, 32768, 128], P('head', 'seq'), may hold values from -32 to 32
- values: bfloat16 [8, 32768, 128], P('head', 'seq'), may hold values from -6 to 6
- grad_out: bfloat16 [8, 32768, 128], P('head', 'seq'), may hold values from -6 to 6
- members: int32 [8, 2, 192, 256], P('head'), may hold values from 0 to 32767, as said below
- counts: int32 [8, 2, 192], P('head'), may hold values from 1 to 256, as said below
Outputs:
- d_qk: bfloat16 [8, 32768, 128], P('head', 'seq')
- d_values: bfloat16 [8, 32768, 128], P('head', 'seq')
The draws below stay inside these ranges and needn't reach their ends.
Inputs may be any that keep to these rules, and one draw needn't show every extreme that they name: `members`: for each head and round, every token index is in exactly one valid slot; the valid slots of a group are its first counts ones and hold increasing tokens, other slots hold any token. The 3 groups c with c // 3 equal hold at most 16 valid slots whose tokens t have one value of t // 512. For each head and round the counts sum to 32768.
All inputs are finite; a program needn't handle non-finite values.
Results may differ from the reference program's by a relative error of at most 0.012.
Values may be sent and summed in bfloat16 or wider, within the bound.
A program may use at most 64 MiB of HBM per device.

```python
import jax
import jax.numpy as jnp
from jax import lax

DH = 128
HEADS = 8
ROUNDS = 2
CAP = 256
TOK_DEV = 512
TOKENS = 32768
CH_DEV = 3
GROUPS = 192


def draw_qk(key, part):
    shape = (HEADS, TOKENS, DH)
    streams = jax.random.split(jax.random.fold_in(key, 3), 1)
    result = 1.5 * jax.random.truncated_normal(streams[0], -4.0, 4.0, shape, jnp.float32)
    return result.astype(jnp.bfloat16)


def route_one(key):
    device_total = TOKENS // TOK_DEV
    half_mean = TOK_DEV // device_total // 2
    streams = jax.random.split(key, 6)
    spread = jax.random.randint(streams[0], (device_total,), 0, half_mean + 1).at[0].set(half_mean).at[1].set(0)
    offset = spread - jnp.roll(spread, -1)
    tilt = jax.random.randint(streams[1], (device_total,), 0, half_mean + 1).at[0].set(half_mean).at[1].set(0)
    tilt_step = tilt - jnp.roll(tilt, -1)
    owners = jnp.arange(device_total, dtype=jnp.int32)
    pair_counts = 2 * half_mean + offset[(owners[:, None] - owners[None, :]) % device_total] + tilt_step[:, None]
    bounds = jnp.cumsum(pair_counts, axis=0)
    ranking = jax.vmap(lambda stream: jax.random.permutation(stream, TOK_DEV))(jax.random.split(streams[2], device_total))
    owner_of = jnp.sum((bounds.T[:, None, :] <= ranking[:, :, None]).astype(jnp.int32), axis=2).reshape(-1)
    order_key = owner_of * TOKENS + jax.random.permutation(streams[3], TOKENS).astype(jnp.int32)
    order = jnp.argsort(order_key).astype(jnp.int32)
    load = jnp.sum(pair_counts, axis=1)
    start = jnp.cumsum(load) - load
    quotient = load // CH_DEV
    remainder = load % CH_DEV
    group_ids = jnp.arange(CH_DEV, dtype=jnp.int32)
    base = quotient[:, None] + (group_ids[None, :] < remainder[:, None]).astype(jnp.int32)
    jitter_top = jnp.maximum(jnp.minimum(jnp.minimum(CAP - quotient - 1, quotient - 1), CAP // 4), 0)
    jitter = jax.random.randint(streams[4], (device_total, CH_DEV), 0, jitter_top[:, None] + 1)
    group_counts = base + jitter - jnp.roll(jitter, -1, axis=1)
    group_start = jnp.cumsum(group_counts, axis=1) - group_counts
    slots = jnp.arange(CAP, dtype=jnp.int32)
    places = start[:, None, None] + group_start[:, :, None] + slots[None, None, :]
    valid = slots[None, None, :] < group_counts[:, :, None]
    tokens_at = order[jnp.clip(places, 0, TOKENS - 1)]
    keyed = jnp.sort(jnp.where(valid, tokens_at, TOKENS + slots[None, None, :]), axis=2)
    filler = jax.random.randint(streams[5], keyed.shape, 0, TOKENS)
    listed = jnp.where(keyed < TOKENS, keyed, filler)
    return (listed.reshape(device_total * CH_DEV, CAP).astype(jnp.int32), group_counts.reshape(-1).astype(jnp.int32))


def routing(key):
    streams = jax.random.split(jax.random.fold_in(key, 7), HEADS * ROUNDS)
    listed, group_counts = lax.map(route_one, streams)
    return (listed.reshape(HEADS, ROUNDS, GROUPS, CAP), group_counts.reshape(HEADS, ROUNDS, GROUPS))


def draw_members(key, part):
    return routing(key)[0]


def draw_counts(key, part):
    return routing(key)[1]


def levels(stream_key, dims, cuts, smallest, high):
    factor_of = 1.0
    for position, parts in cuts:
        heights = jax.random.uniform(jax.random.fold_in(jax.random.fold_in(stream_key, 6), position), (parts,), jnp.float32, smallest / len(cuts), high / len(cuts))
        factor_of = factor_of * jnp.repeat(jnp.exp(heights), dims[position] // parts).reshape((-1,) + (1,) * (len(dims) - 1 - position))
    return factor_of


def scatter_about(rng, extent, scale, limit, shards=(), held_as=jnp.bfloat16):
    values = jax.random.normal(rng, extent, jnp.float32) * scale
    if len(shards) > 0:
        values = levels(rng, extent, shards, -0.22, 0.18) * values
    return jnp.clip(values, min=-limit, max=limit).astype(held_as)


def setup_inputs(seed: int = 0) -> dict:
    streams_of = jax.random.split(jax.random.key(seed), 6)
    return {
        "qk": draw_qk(jax.random.fold_in(streams_of[5], 71), 0),
        "values": scatter_about(streams_of[1], (HEADS, TOKENS, DH), 1.0, 6.0, ((0, 8), (1, 64))),
        "grad_out": scatter_about(streams_of[2], (HEADS, TOKENS, DH), 1.0, 6.0, ((0, 8), (1, 64))),
        "members": draw_members(jax.random.fold_in(streams_of[5], 71), 0),
        "counts": draw_counts(jax.random.fold_in(streams_of[5], 71), 0),
    }


masked_score = -1e+30
norm_eps = 1e-06

def group_forward(queries, key_rows, value_rows, allowed):
    key_float = key_rows.astype(jnp.float32)
    inverse = lax.rsqrt(lax.optimization_barrier(jnp.sum(key_float * key_float, axis=-1, keepdims=True)) + norm_eps)
    unit_keys = (key_float * inverse).astype(jnp.bfloat16)
    scores = jnp.dot(queries, unit_keys.T, preferred_element_type=jnp.float32)
    scores = jnp.where(allowed, scores, masked_score)
    highest = lax.optimization_barrier(jnp.max(scores, axis=-1, keepdims=True))
    log_total = highest + jnp.log(lax.optimization_barrier(jnp.sum(jnp.exp(scores - highest), axis=-1, keepdims=True)))
    probability = jnp.exp(scores - log_total)
    rounded = probability.astype(jnp.bfloat16)
    outputs = jnp.dot(rounded, value_rows, preferred_element_type=jnp.float32)
    return (unit_keys, inverse, probability, rounded, log_total[:, 0], outputs)

def group_backward(queries, key_rows, value_rows, unit_keys, inverse, probability, rounded, out_grad, log_grad):
    d_prob = jnp.dot(out_grad, value_rows.T, preferred_element_type=jnp.float32)
    center = lax.optimization_barrier(jnp.sum(probability * d_prob, axis=-1, keepdims=True))
    d_score = (probability * (d_prob - center + log_grad[:, None])).astype(jnp.bfloat16)
    d_query = jnp.dot(d_score, unit_keys, preferred_element_type=jnp.float32)
    d_unit = jnp.dot(d_score.T, queries, preferred_element_type=jnp.float32)
    key_float = key_rows.astype(jnp.float32)
    cubed = inverse * inverse * inverse
    d_key = inverse * d_unit - key_float * cubed * lax.optimization_barrier(jnp.sum(key_float * d_unit, axis=-1, keepdims=True))
    d_value = jnp.dot(rounded.T, out_grad, preferred_element_type=jnp.float32)
    return (d_query, d_key, d_value)

def head_reference(qk_rows, value_rows, cot_rows, members, counts):
    token_count, feature_size = qk_rows.shape
    rounds, groups, group_size = members.shape
    positions = jnp.arange(group_size, dtype=jnp.int32)
    filled = positions[None, None, :] < counts[:, :, None]
    indices = jnp.where(filled, members, token_count).astype(jnp.int32)

    def padded(rows):
        return jnp.concatenate([rows, jnp.zeros((1, feature_size), rows.dtype)], axis=0)[indices]
    q_slots = padded(qk_rows)
    v_slots = padded(value_rows)
    g_slots = padded(cot_rows)
    q_prev = jnp.roll(q_slots, 1, axis=1)
    v_prev = jnp.roll(v_slots, 1, axis=1)
    fill_prev = jnp.roll(filled, 1, axis=1)
    not_self = jnp.arange(2 * group_size, dtype=jnp.int32)[None, :] != positions[:, None] + group_size

    def flatten(array):
        return array.reshape((rounds * groups,) + array.shape[2:])
    items = (flatten(q_slots), flatten(q_prev), flatten(v_slots), flatten(v_prev), flatten(filled), flatten(fill_prev), flatten(g_slots))

    def prepare(entry):
        queries, prev_q, values_now, prev_v, fill_now, fill_before, cot_now = entry
        key_rows = jnp.concatenate([prev_q, queries], axis=0)
        value_keys = jnp.concatenate([prev_v, values_now], axis=0)
        allowed = jnp.concatenate([fill_before, fill_now], axis=0)[None, :] & not_self
        return (queries, key_rows, value_keys, allowed, cot_now)

    def forward_item(entry):
        queries, key_rows, value_keys, allowed, cot_now = prepare(entry)
        result = group_forward(queries, key_rows, value_keys, allowed)
        dots = lax.optimization_barrier(jnp.sum(cot_now.astype(jnp.float32) * result[5], axis=-1))
        return (result[4], dots)
    log_slots, dot_slots = lax.map(forward_item, items)
    log_slots = log_slots.reshape(rounds, groups, group_size)
    dot_slots = dot_slots.reshape(rounds, groups, group_size)
    round_grid = jnp.broadcast_to(jnp.arange(rounds, dtype=jnp.int32)[:, None, None], indices.shape)

    def to_tokens(slot_values):
        return jnp.zeros((rounds, token_count + 1), jnp.float32).at[round_grid, indices].set(slot_values)[:, :token_count]
    log_tok = to_tokens(log_slots)
    dot_tok = to_tokens(dot_slots)
    highest = lax.optimization_barrier(jnp.max(log_tok, axis=0))
    exponent = jnp.exp(log_tok - highest)
    weight = exponent / lax.optimization_barrier(jnp.sum(exponent, axis=0))
    mixture = lax.optimization_barrier(jnp.sum(weight * dot_tok, axis=0))
    log_grad = weight * (dot_tok - mixture)

    def to_slots(token_values):
        padded_values = jnp.concatenate([token_values, jnp.zeros((rounds, 1), jnp.float32)], axis=1)
        return padded_values[round_grid, indices]
    weight_slots = flatten(to_slots(weight))
    grad_slots = flatten(to_slots(log_grad))

    def backward_item(entry):
        base, weight_now, log_now = entry
        queries, key_rows, value_keys, allowed, cot_now = prepare(base)
        unit_keys, inverse, probability, rounded, log_total, outputs = group_forward(queries, key_rows, value_keys, allowed)
        out_grad = (weight_now[:, None] * cot_now.astype(jnp.float32)).astype(jnp.bfloat16)
        return group_backward(queries, key_rows, value_keys, unit_keys, inverse, probability, rounded, out_grad, log_now)
    d_query, d_key, d_value = lax.map(backward_item, (items, weight_slots, grad_slots))
    d_query = d_query.reshape(rounds, groups, group_size, feature_size)
    d_key = d_key.reshape(rounds, groups, 2 * group_size, feature_size)
    d_value = d_value.reshape(rounds, groups, 2 * group_size, feature_size)
    own_q = d_query + d_key[:, :, group_size:] + jnp.roll(d_key[:, :, :group_size], -1, axis=1)
    own_v = d_value[:, :, group_size:] + jnp.roll(d_value[:, :, :group_size], -1, axis=1)
    flat_index = indices.reshape(-1)
    grad_qk = jnp.zeros((token_count + 1, feature_size), jnp.float32).at[flat_index].add(own_q.reshape(-1, feature_size))
    grad_v = jnp.zeros((token_count + 1, feature_size), jnp.float32).at[flat_index].add(own_v.reshape(-1, feature_size))
    return (grad_qk[:token_count].astype(jnp.bfloat16), grad_v[:token_count].astype(jnp.bfloat16))

def head_item(entry):
    return head_reference(entry[0], entry[1], entry[2], entry[3], entry[4])

def reference(qk, values, grad_out, members, counts):
    d_qk, d_values = lax.map(head_item, (qk, values, grad_out, members, counts))
    return (d_qk, d_values)
```

```python
import functools

import jax
import jax.numpy as jnp
from jax import lax
from jax.experimental import pallas as pl
from jax.experimental.pallas import tpu as pltpu
from jax.sharding import PartitionSpec as P

MESH = pl.DeviceIdType.MESH
F32 = jnp.float32
BF16 = jnp.bfloat16
masked_score = -1e30
norm_eps = 1e-06
NZ = 16
NN = (((1,), (0,)), ((), ()))
NT = (((1,), (1,)), ((), ()))
TN = (((0,), (0,)), ((), ()))


def mm(a, b, dims=NN, precision=None):
    return lax.dot_general(a, b, dims, precision=precision, preferred_element_type=F32)


def exact(a, b, dims=NN):
    return mm(a, b, dims, lax.Precision.HIGHEST)


def iota(shape, axis):
    return lax.broadcasted_iota(jnp.int32, shape, axis)


def kernel(
    n, bound, mt_ref, q_ref, v_ref, g_ref, dq_ref, dv_ref,
    sq, rq, sg, rg, sx, rx, sy, ry, se, re, sb, rb,
    ones_s, ones_o, upper, rt, gt, kv, gs, unit, prob, pdc, d_unit, d_value, d_query,
    send_sem, recv_sem, near_send, near_recv,
):
    me = lax.axis_index("seq")
    tokens, feat = q_ref.shape
    rounds = sq.shape[0]
    slots = mt_ref.shape[1]
    cap = kv.shape[1] - slots
    per = slots // cap
    rows = n * bound
    nx = n // NZ
    following = lax.rem(me + 1, n)
    previous = lax.rem(me + n - 1, n)

    def peer(k):
        a = lax.div(k, nx)
        dx = lax.rem(k, nx) + lax.div(a, NZ - 1)
        dz = NZ // 2 + lax.div(a + 1, 2) * (1 - 2 * lax.rem(a, 2))
        x = lax.rem(lax.div(me, NZ) + dx, nx)
        return x * NZ + lax.rem(me + dz, NZ)

    barrier = pltpu.get_barrier_semaphore()

    def greet(k, carry):
        pl.semaphore_signal(barrier, inc=1, device_id={"seq": peer(k)}, device_id_type=MESH)
        return carry

    lax.fori_loop(0, n - 1, greet, 0)

    def spread(src, dst, idx):
        def one(k, carry):
            to = peer(k)
            pltpu.make_async_remote_copy(
                src_ref=src.at[to],
                dst_ref=dst.at[me],
                send_sem=send_sem.at[idx],
                recv_sem=recv_sem.at[idx],
                device_id={"seq": to},
                device_id_type=MESH,
            ).start()
            return carry

        lax.fori_loop(0, n - 1, one, 0)
        dst[me] = src[me]

    def arrived(dst, idx):
        part = dst.at[pl.ds(0, n - 1)]
        pltpu.make_async_copy(part, part, recv_sem.at[idx]).wait()

    def left(src, idx):
        part = src.at[pl.ds(0, n - 1)]
        pltpu.make_async_copy(part, part, send_sem.at[idx]).wait()

    def near(src, dst, idx, to):
        return pltpu.make_async_remote_copy(
            src_ref=src,
            dst_ref=dst,
            send_sem=near_send.at[idx],
            recv_sem=near_recv.at[idx],
            device_id={"seq": to},
            device_id_type=MESH,
        )

    upper[...] = jnp.where(iota((slots, slots), 0) <= iota((slots, slots), 1), 1.0, 0.0).astype(BF16)
    expand = jnp.where(lax.div(iota((rows, n), 0), bound) == iota((rows, n), 1), 1.0, 0.0).astype(BF16)
    place = (lax.rem(iota((rows, 1), 0), bound) + 1).astype(F32)
    q_v = jnp.concatenate([q_ref[...], v_ref[...]], axis=1)
    for r in range(rounds):
        m = mt_ref[r * n : (r + 1) * n, :]
        mine = lax.div(m + tokens, tokens) - 1 == me
        rank = mm(jnp.where(mine, 1.0, 0.0).astype(BF16), upper[...])
        rank = jnp.where(mine, rank, 0.0)
        local = (m - me * tokens + 1).astype(F32)
        token = (iota((n, tokens), 1) + 1).astype(F32)
        table = jnp.zeros((n, tokens), F32)
        for j in range(1, bound + 1):
            column = jnp.sum(jnp.where(rank == j, local, 0.0), axis=1, keepdims=True)
            table = table + jnp.where(column == token, float(j), 0.0)
        rt[r] = table
        hits = jnp.where(mm(expand, table.astype(BF16)) == place, 1.0, 0.0).astype(BF16)
        ones_s[r] = hits
        sq[r] = mm(hits, q_v).astype(BF16).reshape(n, bound, 2 * feat)
        if r == 0:
            pl.semaphore_wait(barrier, n - 1)
        spread(sq.at[r], rq.at[r], r)
    for r in range(rounds):
        sg[r] = mm(ones_s[r], g_ref[...]).astype(BF16).reshape(n, bound, feat)
        spread(sg.at[r], rg.at[r], 2 + r)

    fill = []
    for r in range(rounds):
        row = mt_ref[pl.ds(r * n + me, 1), :]
        src = lax.div(row + tokens, tokens) - 1
        hit = iota((n, slots), 0) == src
        rank = mm(jnp.where(hit, 1.0, 0.0).astype(BF16), upper[...])
        table = jnp.where(hit, rank, 0.0)
        gt[r] = table
        ones_o[r] = jnp.where(mm(expand, table.astype(BF16)) == place, 1.0, 0.0).astype(BF16)
        before = mt_ref[pl.ds(r * n + previous, 1), :][:, slots - cap :]
        fill.append(jnp.where(jnp.concatenate([before, row], axis=1) >= 0, 1.0, 0.0))
    wide = (128, cap + slots)
    valid = jnp.zeros(wide, F32)
    for r in range(rounds):
        valid = jnp.where(iota(wide, 0) == r, fill[r], valid)
    valid = valid.T

    def normal(k):
        k = k.astype(F32)
        return k, lax.rsqrt(jnp.sum(k * k, axis=1, keepdims=True) + norm_eps)

    def make_unit(r, lo, hi):
        k, inverse = normal(kv[r, lo:hi, :feat])
        unit[r, lo:hi, :] = (k * inverse).astype(BF16)

    for r in range(rounds):
        arrived(rq.at[r], r)
        kv[r, cap:, :] = mm(ones_o[r], rq[r].reshape(rows, 2 * feat), TN).astype(BF16)
        make_unit(r, cap, cap + slots)
        near(kv.at[r, pl.ds(slots, cap)], kv.at[r, pl.ds(0, cap)], r, following).start()

    keep = iota((2 * cap, cap), 0) - cap != iota((2 * cap, cap), 1)
    lse = [[None] * per for _ in range(rounds)]
    dot = [[None] * per for _ in range(rounds)]

    def scores(r, c):
        s = mm(unit[r, c * cap : (c + 2) * cap, :], kv[r, (c + 1) * cap : (c + 2) * cap, :feat], NT)
        ok = keep & (valid[c * cap : (c + 2) * cap, r : r + 1] > 0.0)
        s = jnp.where(ok, s, masked_score)
        high = jnp.max(s, axis=0, keepdims=True)
        e = jnp.exp(s - high)
        total = jnp.sum(e, axis=0, keepdims=True)
        prob[r * per + c] = e * (1.0 / total)
        lse[r][c] = high + jnp.log(total)

    def products(r, c):
        d = mm(kv[r, c * cap : (c + 2) * cap, feat:], gs[r, c * cap : (c + 1) * cap, :], NT)
        p = prob[r * per + c]
        dot[r][c] = jnp.sum(p.astype(BF16).astype(F32) * d, axis=0, keepdims=True)
        center = jnp.sum(p * d, axis=0, keepdims=True)
        pdc[r * per + c] = p * (d - center)

    for r in range(rounds):
        for c in range(1, per):
            scores(r, c)
    for r in range(rounds):
        near(kv.at[r, pl.ds(slots, cap)], kv.at[r, pl.ds(0, cap)], r, following).wait()
        make_unit(r, 0, cap)
        scores(r, 0)
    for r in range(rounds):
        arrived(rg.at[r], 2 + r)
        gs[r] = mm(ones_o[r], rg[r].reshape(rows, feat), TN).astype(BF16)
        for c in range(per):
            products(r, c)

    def lane_of(table, r, kind):
        ranks = jnp.sum(table, axis=0, keepdims=True).astype(jnp.int32) - 1
        ranks = jnp.where(ranks < 0, -128, ranks) + (kind * rounds + r) * bound
        return jnp.where(iota((128, table.shape[1]), 0) == ranks, 1.0, 0.0)

    def pack(tables, values):
        total = jnp.zeros((n, 128), F32)
        for r in range(rounds):
            for kind in range(2):
                spots = jnp.where(tables[r] > 0.0, values[kind][r], 0.0)
                total = total + exact(spots, lane_of(tables[r], r, kind), NT)
        return total

    def unpack(tables, packed):
        out = [[None] * rounds for _ in range(2)]
        for r in range(rounds):
            for kind in range(2):
                spots = exact(packed, lane_of(tables[r], r, kind))
                out[kind][r] = jnp.sum(jnp.where(tables[r] > 0.0, spots, 0.0), axis=0, keepdims=True)
        return out

    slot_tables = [gt[r] for r in range(rounds)]
    token_tables = [rt[r] for r in range(rounds)]
    lse_rows = [jnp.concatenate(lse[r], axis=1) for r in range(rounds)]
    dot_rows = [jnp.concatenate(dot[r], axis=1) for r in range(rounds)]
    sx[:, 0, :] = pack(slot_tables, (lse_rows, dot_rows))
    spread(sx, rx, 4)
    arrived(rx, 4)
    log_tok, dot_tok = unpack(token_tables, rx[:, 0, :])
    highest = functools.reduce(jnp.maximum, log_tok)
    exponent = [jnp.exp(x - highest) for x in log_tok]
    bottom = functools.reduce(jnp.add, exponent)
    weight = [x / bottom for x in exponent]
    mixture = functools.reduce(jnp.add, [w * d for w, d in zip(weight, dot_tok)])
    dlog = [w * (d - mixture) for w, d in zip(weight, dot_tok)]
    sy[:, 0, :] = pack(token_tables, (weight, dlog))
    spread(sy, ry, 5)
    arrived(ry, 5)
    weight, dlog = unpack(slot_tables, ry[:, 0, :])

    def backward(r, c):
        w = weight[r][:, c * cap : (c + 1) * cap]
        p = prob[r * per + c]
        ds = (w * pdc[r * per + c] + dlog[r][:, c * cap : (c + 1) * cap] * p).astype(BF16)
        pw = (w * p).astype(BF16)
        du = mm(ds, kv[r, (c + 1) * cap : (c + 2) * cap, :feat])
        dv = mm(pw, gs[r, c * cap : (c + 1) * cap, :])
        d_query[r, c * cap : (c + 1) * cap, :] = mm(ds, unit[r, c * cap : (c + 2) * cap, :], TN)
        lo, mid, hi = c * cap, (c + 1) * cap, (c + 2) * cap
        if c == 0:
            se[r] = jnp.concatenate([du[:cap], dv[:cap]], axis=1).astype(BF16)
        else:
            d_unit[r, lo:mid, :] += du[:cap]
            d_value[r, lo:mid, :] += dv[:cap]
        d_unit[r, mid:hi, :] = du[cap:]
        d_value[r, mid:hi, :] = dv[cap:]

    for r in range(rounds):
        backward(r, 0)
    for r in range(rounds):
        near(se.at[r], re.at[r], rounds + r, previous).start()
    for r in range(rounds):
        for c in range(1, per):
            backward(r, c)
        near(se.at[r], re.at[r], rounds + r, previous).wait()
        edge = re[r].astype(F32)
        d_unit[r, slots:, :] += edge[:, :feat]
        d_value[r, slots:, :] += edge[:, feat:]
        k, inverse = normal(kv[r, cap:, :feat])
        du = d_unit[r, cap:, :]
        inner = jnp.sum(k * du, axis=1, keepdims=True)
        grad = d_query[r] + inverse * du - k * (inverse * inverse * inverse * inner)
        both = jnp.concatenate([grad, d_value[r, cap:, :]], axis=1).astype(BF16)
        sb[r] = mm(ones_o[r], both).astype(BF16).reshape(n, bound, 2 * feat)
        spread(sb.at[r], rb.at[r], 6 + r)
    total = jnp.zeros((tokens, 2 * feat), F32)
    for r in range(rounds):
        arrived(rb.at[r], 6 + r)
        total = total + mm(ones_s[r], rb[r].reshape(rows, 2 * feat), TN)
    dq_ref[...] = total[:, :feat].astype(BF16)
    dv_ref[...] = total[:, feat:].astype(BF16)
    for r in range(rounds):
        left(sq.at[r], r)
        left(sg.at[r], 2 + r)
        left(sb.at[r], 6 + r)
    left(sx, 4)
    left(sy, 5)


def on_device(qk, values, grad_out, members, counts):
    n = lax.axis_size("seq")
    _, tokens, feat = qk.shape
    _, rounds, groups, cap = members.shape
    slots = groups // n * cap
    bound = 2 * tokens // n
    rows = n * bound
    filled = jnp.arange(cap, dtype=jnp.int32) < counts[0][:, :, None]
    mt = jnp.where(filled, members[0], -1).reshape(rounds * n, slots)
    vmem = pltpu.VMEM
    items = rounds * (groups // n)
    out = jax.ShapeDtypeStruct((tokens, feat), BF16)
    d_qk, d_values = pl.pallas_call(
        functools.partial(kernel, n, bound),
        out_shape=(out, out),
        in_specs=[pl.BlockSpec(memory_space=vmem)] * 4,
        out_specs=(pl.BlockSpec(memory_space=vmem),) * 2,
        scratch_shapes=[
            vmem((rounds, n, bound, 2 * feat), BF16),
            vmem((rounds, n, bound, 2 * feat), BF16),
            vmem((rounds, n, bound, feat), BF16),
            vmem((rounds, n, bound, feat), BF16),
            vmem((n, 1, 128), F32),
            vmem((n, 1, 128), F32),
            vmem((n, 1, 128), F32),
            vmem((n, 1, 128), F32),
            vmem((rounds, cap, 2 * feat), BF16),
            vmem((rounds, cap, 2 * feat), BF16),
            vmem((rounds, n, bound, 2 * feat), BF16),
            vmem((rounds, n, bound, 2 * feat), BF16),
            vmem((rounds, rows, tokens), BF16),
            vmem((rounds, rows, slots), BF16),
            vmem((slots, slots), BF16),
            vmem((rounds, n, tokens), F32),
            vmem((rounds, n, slots), F32),
            vmem((rounds, cap + slots, 2 * feat), BF16),
            vmem((rounds, slots, feat), BF16),
            vmem((rounds, cap + slots, feat), BF16),
            vmem((items, 2 * cap, cap), F32),
            vmem((items, 2 * cap, cap), F32),
            vmem((rounds, cap + slots, feat), F32),
            vmem((rounds, cap + slots, feat), F32),
            vmem((rounds, slots, feat), F32),
            pltpu.SemaphoreType.DMA((8,)),
            pltpu.SemaphoreType.DMA((8,)),
            pltpu.SemaphoreType.DMA((4,)),
            pltpu.SemaphoreType.DMA((4,)),
        ],
        compiler_params=pltpu.CompilerParams(
            collective_id=0, has_side_effects=True, vmem_limit_bytes=60000 * 1024
        ),
        name="lsh_backward",
    )(mt, qk[0], values[0], grad_out[0])
    return d_qk[None], d_values[None]


def solution(mesh):
    rows = P("head", "seq", None)
    return jax.shard_map(
        on_device,
        mesh=mesh,
        in_specs=(rows, rows, rows, P("head", None, None, None), P("head", None, None)),
        out_specs=(rows, rows),
        check_vma=False,
    )
```

```python
import functools

import jax
import jax.numpy as jnp
from jax import lax
from jax.experimental import pallas as pl
from jax.experimental.pallas import tpu as pltpu
from jax.sharding import PartitionSpec as P

MESH = pl.DeviceIdType.MESH
F32 = jnp.float32
BF16 = jnp.bfloat16
masked_score = -1e30
norm_eps = 1e-06
NZ = 16
NN = (((1,), (0,)), ((), ()))
NT = (((1,), (1,)), ((), ()))
TN = (((0,), (0,)), ((), ()))


def mm(a, b, dims=NN, precision=None):
    return lax.dot_general(a, b, dims, precision=precision, preferred_element_type=F32)


def iota(shape, axis):
    return lax.broadcasted_iota(jnp.int32, shape, axis)


def kernel(
    n, bound, members_hbm, counts_hbm, q_hbm, v_hbm, g_hbm, dq_ref, dv_ref,
    members_ref, counts_ref, q_ref, v_ref, g_ref, sq, rq, sg, rg, sx, rx, sy, ry, se, re, sb, rb,
    ones_s, ones_o, upper, hit_t, hit_s, lane_t, lane_s, kv, gs, unit, prob, pdc, d_unit, d_value, d_query,
    send_sem, recv_sem, near_send, near_recv, load_sem, turn,
):
    me = lax.axis_index("seq")
    head = lax.axis_index("head")
    core = lax.rem(head, 2)
    tokens, feat = q_ref.shape
    rounds = sq.shape[0]
    _, groups, cap = members_hbm.shape
    per = groups // n
    slots = per * cap
    rows = n * bound
    nx = n // NZ
    following = lax.rem(me + 1, n)
    previous = lax.rem(me + n - 1, n)

    loads = [
        pltpu.make_async_copy(src, dst, load_sem.at[i])
        for i, (src, dst) in enumerate(
            (
                *(
                    (members_hbm.at[:, :, pl.ds(h * 128, 128)], members_ref.at[h])
                    for h in range(cap // 128)
                ),
                (counts_hbm, counts_ref), (q_hbm, q_ref), (v_hbm, v_ref), (g_hbm, g_ref),
            )
        )
    ]
    for load in loads:
        load.start()
    columns = [lax.rem(lax.div(me, NZ) + dx, nx) * NZ for dx in range(nx)]

    def every_peer(act):
        def ring(a, carry):
            dz = NZ // 2 + lax.div(a + 1, 2) * (1 - 2 * lax.rem(a, 2))
            z = lax.rem(me + dz, NZ)
            for dx in range(nx):
                act(columns[dx] + z)
            return carry

        lax.fori_loop(0, NZ - 1, ring, 0)
        for dx in range(1, nx):
            act(columns[dx] + lax.rem(me, NZ))

    barrier = pltpu.get_barrier_semaphore()
    every_peer(
        lambda to: pl.semaphore_signal(
            barrier, inc=1, device_id={"seq": to}, device_id_type=MESH
        )
    )
    other = {"seq": me, "head": head + 1 - 2 * core}
    pl.semaphore_signal(barrier, inc=1, device_id=other, device_id_type=MESH)

    def spread(src, dst, idx):
        def one(to):
            pltpu.make_async_remote_copy(
                src_ref=src.at[to],
                dst_ref=dst.at[me],
                send_sem=send_sem.at[idx],
                recv_sem=recv_sem.at[idx],
                device_id={"seq": to},
                device_id_type=MESH,
            ).start()

        every_peer(one)
        dst[me] = src[me]

    def arrived(dst, idx):
        part = dst.at[pl.ds(0, n - 1)]
        pltpu.make_async_copy(part, part, recv_sem.at[idx]).wait()

    def left(src, idx):
        part = src.at[pl.ds(0, n - 1)]
        pltpu.make_async_copy(part, part, send_sem.at[idx]).wait()

    def near(src, dst, idx, to):
        return pltpu.make_async_remote_copy(
            src_ref=src,
            dst_ref=dst,
            send_sem=near_send.at[idx],
            recv_sem=near_recv.at[idx],
            device_id={"seq": to},
            device_id_type=MESH,
        )

    upper[...] = jnp.where(iota((slots, slots), 0) <= iota((slots, slots), 1), 1.0, 0.0).astype(BF16)
    expand = jnp.where(lax.div(iota((rows, n), 0), bound) == iota((rows, n), 1), 1.0, 0.0).astype(BF16)
    place = (lax.rem(iota((rows, 1), 0), bound) + 1).astype(F32)
    for load in loads:
        load.wait()
    q_v = jnp.concatenate([q_ref[...], v_ref[...]], axis=1)

    def lanes_of(table):
        ranks = jnp.sum(table, axis=0, keepdims=True).astype(jnp.int32) - 1
        return jnp.where(ranks < 0, -128, ranks)

    def place_send(r):
        parts = []
        for c in range(per):
            counts = jnp.broadcast_to(counts_ref[r : r + 1, :], (n, groups))
            picked = iota((n, groups), 1) == iota((n, groups), 0) * per + c
            count = jnp.sum(jnp.where(picked, counts, 0), axis=1, keepdims=True)
            part = jnp.concatenate(
                [members_ref[h, r, pl.ds(c, n, stride=per), :] for h in range(cap // 128)], axis=1
            )
            parts.append(jnp.where(iota((n, cap), 1) < count, part, -1))
        m = jnp.concatenate(parts, axis=1)
        mine = lax.div(m + tokens, tokens) - 1 == me
        rank = mm(jnp.where(mine, 1.0, 0.0).astype(BF16), upper[...])
        rank = jnp.where(mine, rank, 0.0)
        local = (m - me * tokens + 1).astype(F32)
        token = (iota((n, tokens), 1) + 1).astype(F32)
        table = jnp.zeros((n, tokens), F32)
        for j in range(1, bound + 1):
            column = jnp.sum(jnp.where(rank == j, local, 0.0), axis=1, keepdims=True)
            table = table + jnp.where(column == token, float(j), 0.0)
        hits = jnp.where(mm(expand, table.astype(BF16)) == place, 1.0, 0.0).astype(BF16)
        ones_s[r] = hits
        return table

    for r in range(rounds):
        table = place_send(r)
        sq[r] = mm(ones_s[r], q_v).astype(BF16).reshape(n, bound, 2 * feat)
        if r == 0:
            pl.semaphore_wait(barrier, n)

        @pl.when(core == 0)
        def _():
            spread(sq.at[r], rq.at[r], r)

        hit_t[r] = jnp.where(table > 0.0, 1.0, 0.0).astype(BF16)
        lanes = lanes_of(table) + r * bound
        lane_t[:, r * tokens : (r + 1) * tokens] = jnp.where(
            iota((128, tokens), 0) == lanes, 1.0, 0.0
        ).astype(BF16)
    for r in range(rounds):
        sg[r] = mm(ones_s[r], g_ref[...]).astype(BF16).reshape(n, bound, feat)

    @pl.when(core == 0)
    def _():
        spread(sg.at[0], rg.at[0], 2)

    def own_row(r, group):
        row = jnp.concatenate(
            [members_ref[h, r, pl.ds(group, 1), :] for h in range(cap // 128)], axis=1
        )
        counts = counts_ref[r : r + 1, :]
        count = jnp.sum(jnp.where(iota((1, groups), 1) == group, counts, 0), axis=1, keepdims=True)
        return jnp.where(iota((1, cap), 1) < count, row, -1)

    fill = []
    for r in range(rounds):
        row = jnp.concatenate([own_row(r, me * per + c) for c in range(per)], axis=1)
        src = lax.div(row + tokens, tokens) - 1
        hit = iota((n, slots), 0) == src
        spot = jnp.where(hit, 1.0, 0.0).astype(BF16)
        hit_s[r] = spot
        rank = mm(spot, upper[...])
        table = jnp.where(hit, rank, 0.0)
        ones_o[r] = jnp.where(mm(expand, table.astype(BF16)) == place, 1.0, 0.0).astype(BF16)
        lanes = lanes_of(table) + r * bound
        lane_s[:, r * slots : (r + 1) * slots] = jnp.where(
            iota((128, slots), 0) == lanes, 1.0, 0.0
        ).astype(BF16)
        before = own_row(r, previous * per + per - 1)
        fill.append(jnp.where(jnp.concatenate([before, row], axis=1) >= 0, 1.0, 0.0))
    wide = (128, cap + slots)
    valid = jnp.zeros(wide, F32)
    for r in range(rounds):
        valid = jnp.where(iota(wide, 0) == r, fill[r], valid)
    valid = valid.T

    @pl.when(core == 1)
    def _():
        pl.semaphore_wait(turn, 1)
        for r in range(rounds):
            spread(sq.at[r], rq.at[r], r)
        spread(sg.at[0], rg.at[0], 2)

    def normal(k):
        k = k.astype(F32)
        return k, lax.rsqrt(jnp.sum(k * k, axis=1, keepdims=True) + norm_eps)

    def make_unit(r, lo, hi):
        k, inverse = normal(kv[r, lo:hi, :feat])
        unit[r, lo:hi, :] = (k * inverse).astype(BF16)

    for r in range(rounds):
        arrived(rq.at[r], r)
        kv[r, cap:, :] = mm(ones_o[r], rq[r].reshape(rows, 2 * feat), TN).astype(BF16)
        make_unit(r, cap, cap + slots)
        near(kv.at[r, pl.ds(slots, cap)], kv.at[r, pl.ds(0, cap)], r, following).start()
    for r in range(1, rounds):
        spread(sg.at[r], rg.at[r], 2 + r)

    keep = iota((2 * cap, cap), 0) - cap != iota((2 * cap, cap), 1)
    lse = [[None] * per for _ in range(rounds)]
    dot = [[None] * per for _ in range(rounds)]

    def scores(r, c):
        s = mm(unit[r, c * cap : (c + 2) * cap, :], kv[r, (c + 1) * cap : (c + 2) * cap, :feat], NT)
        ok = keep & (valid[c * cap : (c + 2) * cap, r : r + 1] > 0.0)
        s = jnp.where(ok, s, masked_score)
        high = jnp.max(s, axis=0, keepdims=True)
        e = jnp.exp(s - high)
        total = jnp.sum(e, axis=0, keepdims=True)
        prob[r * per + c] = e * (1.0 / total)
        lse[r][c] = high + jnp.log(total)

    def products(r, c):
        d = mm(kv[r, c * cap : (c + 2) * cap, feat:], gs[r, c * cap : (c + 1) * cap, :], NT)
        p = prob[r * per + c]
        dot[r][c] = jnp.sum(p.astype(BF16).astype(F32) * d, axis=0, keepdims=True)
        center = jnp.sum(p * d, axis=0, keepdims=True)
        pdc[r * per + c] = p * (d - center)

    for r in range(rounds):
        for c in range(1, per):
            scores(r, c)

    def look_back(r):
        near(kv.at[r, pl.ds(slots, cap)], kv.at[r, pl.ds(0, cap)], r, following).wait()
        make_unit(r, 0, cap)
        scores(r, 0)

    def cotangents(r):
        arrived(rg.at[r], 2 + r)
        gs[r] = mm(ones_o[r], rg[r].reshape(rows, feat), TN).astype(BF16)

    for r in range(rounds - 1):
        cotangents(r)
        if r == rounds - 2:
            @pl.when(core == 0)
            def _():
                pl.semaphore_signal(turn, inc=1, device_id=other, device_id_type=MESH)

        for c in range(1, per):
            products(r, c)
        look_back(r)
        products(r, 0)
    look_back(rounds - 1)
    cotangents(rounds - 1)
    for c in range(per):
        products(rounds - 1, c)

    shift = rounds * bound

    def split(x):
        high = x.astype(BF16)
        rest = x - high.astype(F32)
        mid = rest.astype(BF16)
        return high, mid, (rest - mid.astype(F32)).astype(BF16)

    def pack(hits, lanes, values):
        blocks = []
        for rows_of in values:
            parts = [split(row) for row in rows_of]
            for i in range(3):
                blocks.append(
                    jnp.concatenate([hits[r] * parts[r][i] for r in range(rounds)], axis=1)
                )
        spread_out = mm(jnp.concatenate(blocks, axis=0), lanes[...], NT)
        first, second = [
            spread_out[i : i + n] + spread_out[i + n : i + 2 * n] + spread_out[i + 2 * n : i + 3 * n]
            for i in (0, 3 * n)
        ]
        return first + pltpu.roll(second, shift, 1)

    def unpack(hits, lanes, packed):
        blocks = split(packed) + split(pltpu.roll(packed, 128 - shift, 1))
        blocks = jnp.concatenate(blocks, axis=0)
        out = [[None] * rounds for _ in range(2)]
        width = lanes.shape[1] // rounds
        for r in range(rounds):
            spots = mm(blocks, lanes[:, r * width : (r + 1) * width])
            for kind in range(2):
                i = 3 * n * kind
                found = spots[i : i + n] + spots[i + n : i + 2 * n] + spots[i + 2 * n : i + 3 * n]
                found = found * hits[r].astype(F32)
                out[kind][r] = jnp.sum(found, axis=0, keepdims=True)
        return out

    lse_rows = [jnp.concatenate(lse[r], axis=1) for r in range(rounds)]
    dot_rows = [jnp.concatenate(dot[r], axis=1) for r in range(rounds)]
    sx[:, 0, :] = pack(hit_s, lane_s, (lse_rows, dot_rows))
    spread(sx, rx, 4)
    arrived(rx, 4)
    log_tok, dot_tok = unpack(hit_t, lane_t, rx[:, 0, :])
    highest = functools.reduce(jnp.maximum, log_tok)
    exponent = [jnp.exp(x - highest) for x in log_tok]
    bottom = functools.reduce(jnp.add, exponent)
    weight = [x / bottom for x in exponent]
    mixture = functools.reduce(jnp.add, [w * d for w, d in zip(weight, dot_tok)])
    dlog = [w * (d - mixture) for w, d in zip(weight, dot_tok)]
    sy[:, 0, :] = pack(hit_t, lane_t, (weight, dlog))
    spread(sy, ry, 5)
    arrived(ry, 5)
    weight, dlog = unpack(hit_s, lane_s, ry[:, 0, :])

    def backward(r, c):
        w = weight[r][:, c * cap : (c + 1) * cap]
        p = prob[r * per + c]
        ds = (w * pdc[r * per + c] + dlog[r][:, c * cap : (c + 1) * cap] * p).astype(BF16)
        pw = (w * p).astype(BF16)
        du = mm(ds, kv[r, (c + 1) * cap : (c + 2) * cap, :feat])
        dv = mm(pw, gs[r, c * cap : (c + 1) * cap, :])
        d_query[r, c * cap : (c + 1) * cap, :] = mm(ds, unit[r, c * cap : (c + 2) * cap, :], TN)
        lo, mid, hi = c * cap, (c + 1) * cap, (c + 2) * cap
        if c == 0:
            se[r] = jnp.concatenate([du[:cap], dv[:cap]], axis=1).astype(BF16)
        else:
            d_unit[r, lo:mid, :] += du[:cap]
            d_value[r, lo:mid, :] += dv[:cap]
        d_unit[r, mid:hi, :] = du[cap:]
        d_value[r, mid:hi, :] = dv[cap:]

    for r in range(rounds):
        backward(r, 0)
    for r in range(rounds):
        near(se.at[r], re.at[r], rounds + r, previous).start()
    for r in range(rounds):
        for c in range(1, per):
            backward(r, c)
        near(se.at[r], re.at[r], rounds + r, previous).wait()
        edge = re[r].astype(F32)
        d_unit[r, slots:, :] += edge[:, :feat]
        d_value[r, slots:, :] += edge[:, feat:]
        k, inverse = normal(kv[r, cap:, :feat])
        du = d_unit[r, cap:, :]
        inner = jnp.sum(k * du, axis=1, keepdims=True)
        grad = d_query[r] + inverse * du - k * (inverse * inverse * inverse * inner)
        both = jnp.concatenate([grad, d_value[r, cap:, :]], axis=1).astype(BF16)
        sb[r] = mm(ones_o[r], both).astype(BF16).reshape(n, bound, 2 * feat)
        spread(sb.at[r], rb.at[r], 6 + r)
    total = jnp.zeros((tokens, 2 * feat), F32)
    for r in range(rounds):
        arrived(rb.at[r], 6 + r)
        total = total + mm(ones_s[r], rb[r].reshape(rows, 2 * feat), TN)
    dq_ref[...] = total[:, :feat].astype(BF16)
    dv_ref[...] = total[:, feat:].astype(BF16)
    for r in range(rounds):
        left(sq.at[r], r)
        left(sg.at[r], 2 + r)
        left(sb.at[r], 6 + r)
    left(sx, 4)
    left(sy, 5)


def on_device(qk, values, grad_out, members, counts):
    n = lax.axis_size("seq")
    _, tokens, feat = qk.shape
    _, rounds, groups, cap = members.shape
    slots = groups // n * cap
    bound = 2 * tokens // n
    rows = n * bound
    vmem = pltpu.VMEM
    items = rounds * (groups // n)
    out = jax.ShapeDtypeStruct((tokens, feat), BF16)
    d_qk, d_values = pl.pallas_call(
        functools.partial(kernel, n, bound),
        out_shape=(out, out),
        in_specs=[pl.BlockSpec(memory_space=pltpu.HBM)] * 5,
        out_specs=(pl.BlockSpec(memory_space=vmem),) * 2,
        scratch_shapes=[
            vmem((cap // 128, rounds, groups, 128), jnp.int32),
            vmem((rounds, groups), jnp.int32),
            vmem((tokens, feat), BF16),
            vmem((tokens, feat), BF16),
            vmem((tokens, feat), BF16),
            vmem((rounds, n, bound, 2 * feat), BF16),
            vmem((rounds, n, bound, 2 * feat), BF16),
            vmem((rounds, n, bound, feat), BF16),
            vmem((rounds, n, bound, feat), BF16),
            vmem((n, 1, 128), F32),
            vmem((n, 1, 128), F32),
            vmem((n, 1, 128), F32),
            vmem((n, 1, 128), F32),
            vmem((rounds, cap, 2 * feat), BF16),
            vmem((rounds, cap, 2 * feat), BF16),
            vmem((rounds, n, bound, 2 * feat), BF16),
            vmem((rounds, n, bound, 2 * feat), BF16),
            vmem((rounds, rows, tokens), BF16),
            vmem((rounds, rows, slots), BF16),
            vmem((slots, slots), BF16),
            vmem((rounds, n, tokens), BF16),
            vmem((rounds, n, slots), BF16),
            vmem((128, rounds * tokens), BF16),
            vmem((128, rounds * slots), BF16),
            vmem((rounds, cap + slots, 2 * feat), BF16),
            vmem((rounds, slots, feat), BF16),
            vmem((rounds, cap + slots, feat), BF16),
            vmem((items, 2 * cap, cap), F32),
            vmem((items, 2 * cap, cap), F32),
            vmem((rounds, cap + slots, feat), F32),
            vmem((rounds, cap + slots, feat), F32),
            vmem((rounds, slots, feat), F32),
            pltpu.SemaphoreType.DMA((8,)),
            pltpu.SemaphoreType.DMA((8,)),
            pltpu.SemaphoreType.DMA((4,)),
            pltpu.SemaphoreType.DMA((4,)),
            pltpu.SemaphoreType.DMA((4 + cap // 128,)),
            pltpu.SemaphoreType.REGULAR,
        ],
        compiler_params=pltpu.CompilerParams(
            collective_id=0, has_side_effects=True, vmem_limit_bytes=66000000
        ),
        name="lsh_backward",
    )(members[0], counts[0], qk[0], values[0], grad_out[0])
    return d_qk[None], d_values[None]


def solution(mesh):
    rows = P("head", "seq", None)
    return jax.shard_map(
        on_device,
        mesh=mesh,
        in_specs=(rows, rows, rows, P("head", None, None, None), P("head", None, None)),
        out_specs=(rows, rows),
        check_vma=False,
    )
```

```python
import functools

import jax
import jax.numpy as jnp
from jax import lax
from jax.experimental import pallas as pl
from jax.experimental.pallas import tpu as pltpu
from jax.sharding import PartitionSpec as P

MESH = pl.DeviceIdType.MESH
F32 = jnp.float32
BF16 = jnp.bfloat16
masked_score = -1e30
norm_eps = 1e-06
NZ = 16
NN = (((1,), (0,)), ((), ()))
NT = (((1,), (1,)), ((), ()))
TN = (((0,), (0,)), ((), ()))


def mm(a, b, dims=NN, precision=None):
    return lax.dot_general(a, b, dims, precision=precision, preferred_element_type=F32)


def iota(shape, axis):
    return lax.broadcasted_iota(jnp.int32, shape, axis)


def kernel(
    n, bound, members_hbm, counts_hbm, q_hbm, v_hbm, g_hbm, dq_ref, dv_ref,
    members_ref, counts_ref, q_ref, v_ref, g_ref, sq, rq, sg, rg, sx, rx, sy, ry, se, re, sb, rb,
    ones_s, ones_o, upper, hit_t, hit_s, lane_t, lane_s, kv, gs, unit, prob, pdc, d_unit, d_value, d_query,
    send_sem, recv_sem, near_send, near_recv, load_sem, turn,
):
    me = lax.axis_index("seq")
    head = lax.axis_index("head")
    core = lax.rem(head, 2)
    tokens, feat = q_ref.shape
    rounds = sq.shape[0]
    _, groups, cap = members_hbm.shape
    per = groups // n
    slots = per * cap
    rows = n * bound
    nx = n // NZ
    following = lax.rem(me + 1, n)
    previous = lax.rem(me + n - 1, n)

    loads = [
        pltpu.make_async_copy(src, dst, load_sem.at[i])
        for i, (src, dst) in enumerate(
            (
                *(
                    (members_hbm.at[:, :, pl.ds(h * 128, 128)], members_ref.at[h])
                    for h in range(cap // 128)
                ),
                (counts_hbm, counts_ref), (q_hbm, q_ref), (v_hbm, v_ref), (g_hbm, g_ref),
            )
        )
    ]
    for load in loads:
        load.start()
    columns = [lax.rem(lax.div(me, NZ) + dx, nx) * NZ for dx in range(nx)]

    def every_peer(act):
        def ring(a, carry):
            dz = NZ // 2 + lax.div(a + 1, 2) * (1 - 2 * lax.rem(a, 2))
            z = lax.rem(me + dz, NZ)
            for dx in range(nx):
                act(columns[dx] + z)
            return carry

        lax.fori_loop(0, NZ - 1, ring, 0)
        for dx in range(1, nx):
            act(columns[dx] + lax.rem(me, NZ))

    barrier = pltpu.get_barrier_semaphore()
    every_peer(
        lambda to: pl.semaphore_signal(
            barrier, inc=1, device_id={"seq": to}, device_id_type=MESH
        )
    )
    other = {"seq": me, "head": head + 1 - 2 * core}
    pl.semaphore_signal(barrier, inc=1, device_id=other, device_id_type=MESH)

    def spread(src, dst, idx):
        def one(to):
            pltpu.make_async_remote_copy(
                src_ref=src.at[to],
                dst_ref=dst.at[me],
                send_sem=send_sem.at[idx],
                recv_sem=recv_sem.at[idx],
                device_id={"seq": to},
                device_id_type=MESH,
            ).start()

        every_peer(one)
        dst[me] = src[me]

    def arrived(dst, idx):
        part = dst.at[pl.ds(0, n - 1)]
        pltpu.make_async_copy(part, part, recv_sem.at[idx]).wait()

    def left(src, idx):
        part = src.at[pl.ds(0, n - 1)]
        pltpu.make_async_copy(part, part, send_sem.at[idx]).wait()

    def near(src, dst, idx, to):
        return pltpu.make_async_remote_copy(
            src_ref=src,
            dst_ref=dst,
            send_sem=near_send.at[idx],
            recv_sem=near_recv.at[idx],
            device_id={"seq": to},
            device_id_type=MESH,
        )

    upper[...] = jnp.where(iota((slots, slots), 0) <= iota((slots, slots), 1), 1.0, 0.0).astype(BF16)
    expand = jnp.where(lax.div(iota((rows, n), 0), bound) == iota((rows, n), 1), 1.0, 0.0).astype(BF16)
    place = (lax.rem(iota((rows, 1), 0), bound) + 1).astype(F32)
    for load in loads:
        load.wait()
    q_v = jnp.concatenate([q_ref[...], v_ref[...]], axis=1)

    def lanes_of(table):
        ranks = jnp.sum(table, axis=0, keepdims=True).astype(jnp.int32) - 1
        return jnp.where(ranks < 0, -128, ranks)

    def place_send(r):
        parts = []
        for c in range(per):
            counts = jnp.broadcast_to(counts_ref[r : r + 1, :], (n, groups))
            picked = iota((n, groups), 1) == iota((n, groups), 0) * per + c
            count = jnp.sum(jnp.where(picked, counts, 0), axis=1, keepdims=True)
            part = jnp.concatenate(
                [members_ref[h, r, pl.ds(c, n, stride=per), :] for h in range(cap // 128)], axis=1
            )
            parts.append(jnp.where(iota((n, cap), 1) < count, part, -1))
        m = jnp.concatenate(parts, axis=1)
        mine = lax.div(m + tokens, tokens) - 1 == me
        rank = mm(jnp.where(mine, 1.0, 0.0).astype(BF16), upper[...])
        rank = jnp.where(mine, rank, 0.0)
        local = (m - me * tokens + 1).astype(F32)
        token = (iota((n, tokens), 1) + 1).astype(F32)
        table = jnp.zeros((n, tokens), F32)
        for j in range(1, bound + 1):
            column = jnp.sum(jnp.where(rank == j, local, 0.0), axis=1, keepdims=True)
            table = table + jnp.where(column == token, float(j), 0.0)
        hits = jnp.where(mm(expand, table.astype(BF16)) == place, 1.0, 0.0).astype(BF16)
        ones_s[r] = hits
        return table

    for r in range(rounds):
        table = place_send(r)
        sq[r] = mm(ones_s[r], q_v).astype(BF16).reshape(n, bound, 2 * feat)
        if r == 0:
            pl.semaphore_wait(barrier, n)

        @pl.when(core == 0)
        def _():
            spread(sq.at[r], rq.at[r], r)

        hit_t[r] = jnp.where(table > 0.0, 1.0, 0.0).astype(BF16)
        lanes = lanes_of(table) + r * bound
        lane_t[:, r * tokens : (r + 1) * tokens] = jnp.where(
            iota((128, tokens), 0) == lanes, 1.0, 0.0
        ).astype(BF16)
    for r in range(rounds):
        sg[r] = mm(ones_s[r], g_ref[...]).astype(BF16).reshape(n, bound, feat)

    @pl.when(core == 0)
    def _():
        spread(sg.at[0], rg.at[0], 2)

    def own_row(r, group):
        row = jnp.concatenate(
            [members_ref[h, r, pl.ds(group, 1), :] for h in range(cap // 128)], axis=1
        )
        counts = counts_ref[r : r + 1, :]
        count = jnp.sum(jnp.where(iota((1, groups), 1) == group, counts, 0), axis=1, keepdims=True)
        return jnp.where(iota((1, cap), 1) < count, row, -1)

    fill = []
    for r in range(rounds):
        row = jnp.concatenate([own_row(r, me * per + c) for c in range(per)], axis=1)
        src = lax.div(row + tokens, tokens) - 1
        hit = iota((n, slots), 0) == src
        spot = jnp.where(hit, 1.0, 0.0).astype(BF16)
        hit_s[r] = spot
        rank = mm(spot, upper[...])
        table = jnp.where(hit, rank, 0.0)
        ones_o[r] = jnp.where(mm(expand, table.astype(BF16)) == place, 1.0, 0.0).astype(BF16)
        lanes = lanes_of(table) + r * bound
        lane_s[:, r * slots : (r + 1) * slots] = jnp.where(
            iota((128, slots), 0) == lanes, 1.0, 0.0
        ).astype(BF16)
        before = own_row(r, previous * per + per - 1)
        fill.append(jnp.where(jnp.concatenate([before, row], axis=1) >= 0, 1.0, 0.0))
    wide = (128, cap + slots)
    valid = jnp.zeros(wide, F32)
    for r in range(rounds):
        valid = jnp.where(iota(wide, 0) == r, fill[r], valid)
    valid = valid.T

    @pl.when(core == 1)
    def _():
        pl.semaphore_wait(turn, 1)
        for r in range(rounds):
            spread(sq.at[r], rq.at[r], r)
        spread(sg.at[0], rg.at[0], 2)

    def normal(k):
        k = k.astype(F32)
        return k, lax.rsqrt(jnp.sum(k * k, axis=1, keepdims=True) + norm_eps)

    def make_unit(r, lo, hi):
        k, inverse = normal(kv[r, lo:hi, :feat])
        unit[r, lo:hi, :] = (k * inverse).astype(BF16)

    for r in range(rounds):
        arrived(rq.at[r], r)
        kv[r, cap:, :] = mm(ones_o[r], rq[r].reshape(rows, 2 * feat), TN).astype(BF16)
        make_unit(r, cap, cap + slots)
        near(kv.at[r, pl.ds(slots, cap)], kv.at[r, pl.ds(0, cap)], r, following).start()
    for r in range(1, rounds):
        spread(sg.at[r], rg.at[r], 2 + r)

    keep = iota((2 * cap, cap), 0) - cap != iota((2 * cap, cap), 1)
    lse = [[None] * per for _ in range(rounds)]
    dot = [[None] * per for _ in range(rounds)]

    def scores(r, c):
        s = mm(unit[r, c * cap : (c + 2) * cap, :], kv[r, (c + 1) * cap : (c + 2) * cap, :feat], NT)
        ok = keep & (valid[c * cap : (c + 2) * cap, r : r + 1] > 0.0)
        s = jnp.where(ok, s, masked_score)
        high = jnp.max(s, axis=0, keepdims=True)
        e = jnp.exp(s - high)
        total = jnp.sum(e, axis=0, keepdims=True)
        prob[r * per + c] = e * (1.0 / total)
        lse[r][c] = high + jnp.log(total)

    def products(r, c):
        d = mm(kv[r, c * cap : (c + 2) * cap, feat:], gs[r, c * cap : (c + 1) * cap, :], NT)
        p = prob[r * per + c]
        dot[r][c] = jnp.sum(p.astype(BF16).astype(F32) * d, axis=0, keepdims=True)
        center = jnp.sum(p * d, axis=0, keepdims=True)
        pdc[r * per + c] = p * (d - center)

    for r in range(rounds):
        for c in range(1, per):
            scores(r, c)

    def look_back(r):
        near(kv.at[r, pl.ds(slots, cap)], kv.at[r, pl.ds(0, cap)], r, following).wait()
        make_unit(r, 0, cap)
        scores(r, 0)

    def cotangents(r):
        arrived(rg.at[r], 2 + r)
        gs[r] = mm(ones_o[r], rg[r].reshape(rows, feat), TN).astype(BF16)

    for r in range(rounds - 1):
        cotangents(r)
        if r == rounds - 2:
            @pl.when(core == 0)
            def _():
                pl.semaphore_signal(turn, inc=1, device_id=other, device_id_type=MESH)

        for c in range(1, per):
            products(r, c)
        look_back(r)
        products(r, 0)
    look_back(rounds - 1)
    cotangents(rounds - 1)
    for c in range(per):
        products(rounds - 1, c)

    shift = rounds * bound

    def split(x):
        high = x.astype(BF16)
        rest = x - high.astype(F32)
        mid = rest.astype(BF16)
        return high, mid, (rest - mid.astype(F32)).astype(BF16)

    def pack(hits, lanes, values):
        blocks = []
        for rows_of in values:
            parts = [split(row) for row in rows_of]
            for i in range(3):
                blocks.append(
                    jnp.concatenate([hits[r] * parts[r][i] for r in range(rounds)], axis=1)
                )
        spread_out = mm(jnp.concatenate(blocks, axis=0), lanes[...], NT)
        first, second = [
            spread_out[i : i + n] + spread_out[i + n : i + 2 * n] + spread_out[i + 2 * n : i + 3 * n]
            for i in (0, 3 * n)
        ]
        return first + pltpu.roll(second, shift, 1)

    def unpack(hits, lanes, packed):
        blocks = split(packed) + split(pltpu.roll(packed, 128 - shift, 1))
        blocks = jnp.concatenate(blocks, axis=0)
        out = [[None] * rounds for _ in range(2)]
        width = lanes.shape[1] // rounds
        for r in range(rounds):
            spots = mm(blocks, lanes[:, r * width : (r + 1) * width])
            for kind in range(2):
                i = 3 * n * kind
                found = spots[i : i + n] + spots[i + n : i + 2 * n] + spots[i + 2 * n : i + 3 * n]
                found = found * hits[r].astype(F32)
                out[kind][r] = jnp.sum(found, axis=0, keepdims=True)
        return out

    lse_rows = [jnp.concatenate(lse[r], axis=1) for r in range(rounds)]
    dot_rows = [jnp.concatenate(dot[r], axis=1) for r in range(rounds)]
    sx[:, 0, :] = pack(hit_s, lane_s, (lse_rows, dot_rows))
    spread(sx, rx, 4)
    arrived(rx, 4)
    log_tok, dot_tok = unpack(hit_t, lane_t, rx[:, 0, :])
    highest = functools.reduce(jnp.maximum, log_tok)
    exponent = [jnp.exp(x - highest) for x in log_tok]
    bottom = functools.reduce(jnp.add, exponent)
    weight = [x / bottom for x in exponent]
    mixture = functools.reduce(jnp.add, [w * d for w, d in zip(weight, dot_tok)])
    dlog = [w * (d - mixture) for w, d in zip(weight, dot_tok)]
    sy[:, 0, :] = pack(hit_t, lane_t, (weight, dlog))
    spread(sy, ry, 5)
    arrived(ry, 5)
    weight, dlog = unpack(hit_s, lane_s, ry[:, 0, :])

    def backward(r, c):
        w = weight[r][:, c * cap : (c + 1) * cap]
        p = prob[r * per + c]
        ds = (w * pdc[r * per + c] + dlog[r][:, c * cap : (c + 1) * cap] * p).astype(BF16)
        pw = (w * p).astype(BF16)
        du = mm(ds, kv[r, (c + 1) * cap : (c + 2) * cap, :feat])
        dv = mm(pw, gs[r, c * cap : (c + 1) * cap, :])
        d_query[r, c * cap : (c + 1) * cap, :] = mm(ds, unit[r, c * cap : (c + 2) * cap, :], TN)
        lo, mid, hi = c * cap, (c + 1) * cap, (c + 2) * cap
        if c == 0:
            se[r] = jnp.concatenate([du[:cap], dv[:cap]], axis=1).astype(BF16)
        else:
            d_unit[r, lo:mid, :] += du[:cap]
            d_value[r, lo:mid, :] += dv[:cap]
        d_unit[r, mid:hi, :] = du[cap:]
        d_value[r, mid:hi, :] = dv[cap:]

    for r in range(rounds):
        backward(r, 0)
        near(se.at[r], re.at[r], rounds + r, previous).start()
    for r in range(rounds):
        for c in range(1, per):
            backward(r, c)
        near(se.at[r], re.at[r], rounds + r, previous).wait()
        edge = re[r].astype(F32)
        d_unit[r, slots:, :] += edge[:, :feat]
        d_value[r, slots:, :] += edge[:, feat:]
        k, inverse = normal(kv[r, cap:, :feat])
        du = d_unit[r, cap:, :]
        inner = jnp.sum(k * du, axis=1, keepdims=True)
        grad = d_query[r] + inverse * du - k * (inverse * inverse * inverse * inner)
        both = jnp.concatenate([grad, d_value[r, cap:, :]], axis=1).astype(BF16)
        sb[r] = mm(ones_o[r], both).astype(BF16).reshape(n, bound, 2 * feat)
        spread(sb.at[r], rb.at[r], 6 + r)
    total = jnp.zeros((tokens, 2 * feat), F32)
    for r in range(rounds):
        arrived(rb.at[r], 6 + r)
        total = total + mm(ones_s[r], rb[r].reshape(rows, 2 * feat), TN)
    dq_ref[...] = total[:, :feat].astype(BF16)
    dv_ref[...] = total[:, feat:].astype(BF16)
    for r in range(rounds):
        left(sq.at[r], r)
        left(sg.at[r], 2 + r)
        left(sb.at[r], 6 + r)
    left(sx, 4)
    left(sy, 5)


def on_device(qk, values, grad_out, members, counts):
    n = lax.axis_size("seq")
    _, tokens, feat = qk.shape
    _, rounds, groups, cap = members.shape
    slots = groups // n * cap
    bound = 2 * tokens // n
    rows = n * bound
    vmem = pltpu.VMEM
    items = rounds * (groups // n)
    out = jax.ShapeDtypeStruct((tokens, feat), BF16)
    d_qk, d_values = pl.pallas_call(
        functools.partial(kernel, n, bound),
        out_shape=(out, out),
        in_specs=[pl.BlockSpec(memory_space=pltpu.HBM)] * 5,
        out_specs=(pl.BlockSpec(memory_space=vmem),) * 2,
        scratch_shapes=[
            vmem((cap // 128, rounds, groups, 128), jnp.int32),
            vmem((rounds, groups), jnp.int32),
            vmem((tokens, feat), BF16),
            vmem((tokens, feat), BF16),
            vmem((tokens, feat), BF16),
            vmem((rounds, n, bound, 2 * feat), BF16),
            vmem((rounds, n, bound, 2 * feat), BF16),
            vmem((rounds, n, bound, feat), BF16),
            vmem((rounds, n, bound, feat), BF16),
            vmem((n, 1, 128), F32),
            vmem((n, 1, 128), F32),
            vmem((n, 1, 128), F32),
            vmem((n, 1, 128), F32),
            vmem((rounds, cap, 2 * feat), BF16),
            vmem((rounds, cap, 2 * feat), BF16),
            vmem((rounds, n, bound, 2 * feat), BF16),
            vmem((rounds, n, bound, 2 * feat), BF16),
            vmem((rounds, rows, tokens), BF16),
            vmem((rounds, rows, slots), BF16),
            vmem((slots, slots), BF16),
            vmem((rounds, n, tokens), BF16),
            vmem((rounds, n, slots), BF16),
            vmem((128, rounds * tokens), BF16),
            vmem((128, rounds * slots), BF16),
            vmem((rounds, cap + slots, 2 * feat), BF16),
            vmem((rounds, slots, feat), BF16),
            vmem((rounds, cap + slots, feat), BF16),
            vmem((items, 2 * cap, cap), F32),
            vmem((items, 2 * cap, cap), F32),
            vmem((rounds, cap + slots, feat), F32),
            vmem((rounds, cap + slots, feat), F32),
            vmem((rounds, slots, feat), F32),
            pltpu.SemaphoreType.DMA((8,)),
            pltpu.SemaphoreType.DMA((8,)),
            pltpu.SemaphoreType.DMA((4,)),
            pltpu.SemaphoreType.DMA((4,)),
            pltpu.SemaphoreType.DMA((4 + cap // 128,)),
            pltpu.SemaphoreType.REGULAR,
        ],
        compiler_params=pltpu.CompilerParams(
            collective_id=0, has_side_effects=True, vmem_limit_bytes=36 * 1024 * 1024
        ),
        name="lsh_backward",
    )(
        *(
            pltpu.with_memory_space_constraint(x[0], pltpu.HBM)
            for x in (members, counts, qk, values, grad_out)
        )
    )
    return d_qk[None], d_values[None]


def solution(mesh):
    rows = P("head", "seq", None)
    return jax.shard_map(
        on_device,
        mesh=mesh,
        in_specs=(rows, rows, rows, P("head", None, None, None), P("head", None, None)),
        out_specs=(rows, rows),
        check_vma=False,
    )
```
